256 devices in a mesh: context: 16 (over z, core), heads: 16 (over x, y).
Axes of the slice: x: 4, y: 4, z: 8, core: 2. Of those that a mesh axis runs over, the one named last changes fastest.
Arguments:
- main_query: bfloat16 [256, 128, 576], P('context', 'heads'), may hold values from -6 to 6
- latent_keys: bfloat16 [32768, 576], P('context'), may hold values from -6 to 6
- head_lse: float32 [256, 128], P(None, 'heads'), may hold values from 4 to 8
- lengths: int32 [256], replicated, may hold values from 1 to 32768, as said below
- index_query: bfloat16 [256, 64, 128], P('heads'), may hold values from -256 to 256
- index_key: bfloat16 [32768, 128], P('context'), may hold values from -8 to 8
- index_weight: float32 [256, 64], P('heads'), may hold values from -2.4 to 2.4
Outputs:
- grad_index_query: float32 [256, 64, 128], P('heads', 'context')
- grad_index_key: float32 [32768, 128], P(('context', 'heads'))
The draws below stay inside these ranges and needn't reach their ends.
Inputs may be any that keep to these rules, and one draw needn't show every extreme that they name: Query rows come in blocks of 16 consecutive rows whose lengths rise by one from row to row; some block ends at the last key.
All inputs are finite; a program needn't handle non-finite values.
Results may differ from the reference program's by a relative error of at most 0.0029.
Values may be sent and summed in bfloat16 or wider, within the bound.
A program may use at most 64 MiB of HBM per device.

```python
import math
import jax
import jax.numpy as jnp
from jax import lax

HEADS = 128
LATENT = 576
IDX_HEADS = 64
IDX_DIM = 128
GROUP = 16
QUERIES = 256
KEYS = 32768


def index_draws(key):
    base = jax.random.fold_in(key, 4099)
    key_query, key_keys, key_weight = jax.random.split(base, 3)
    query_vals = jnp.clip(jax.random.normal(key_query, (QUERIES, IDX_HEADS, IDX_DIM), jnp.float32), -4.0, 4.0)
    key_vals = jnp.clip(jax.random.normal(key_keys, (KEYS, IDX_DIM), jnp.float32), -4.0, 4.0)
    weight_vals = jnp.clip(0.6 * jax.random.normal(key_weight, (QUERIES, IDX_HEADS), jnp.float32), -2.4, 2.4)
    query_vals = query_vals.astype(jnp.bfloat16).astype(jnp.float32)
    key_vals = key_vals.astype(jnp.bfloat16).astype(jnp.float32)
    return (query_vals, key_vals, weight_vals)


def draw_index_query(key, part):
    return index_draws(key)[0].astype(jnp.bfloat16)


def draw_index_key(key, part):
    return index_draws(key)[1].astype(jnp.bfloat16)


def draw_index_weight(key, part):
    return index_draws(key)[2]


def draw_lengths(key, part):
    group_total = QUERIES // GROUP
    key_offset, key_first = jax.random.split(jax.random.fold_in(key, 1201), 2)
    offsets = jax.random.randint(key_offset, (group_total,), 0, KEYS - GROUP + 1, dtype=jnp.int32)
    first_group = jax.random.randint(key_first, (), 0, group_total, dtype=jnp.int32)
    offsets = offsets.at[first_group].set(KEYS - GROUP)
    within = jnp.arange(QUERIES, dtype=jnp.int32)
    return offsets[within // GROUP] + within % GROUP + 1


def shard_levels(own_key, dims, pieces, low, largest):
    level, own = 1.0, jax.random.fold_in(own_key, 6)
    for position, blocks in pieces:
        draws = jnp.exp(jax.random.uniform(jax.random.fold_in(own, position), (blocks,), jnp.float32, low / len(pieces), largest / len(pieces)))
        level = level * jnp.repeat(draws, dims[position] // blocks).reshape([-1 if axis == position else 1 for axis in range(len(dims))])
    return level


def scatter_about(key, shape, deviation, limit, pieces=(), kind=jnp.bfloat16):
    values = jax.random.normal(key, shape, jnp.float32) * deviation
    if len(pieces) > 0:
        values = shard_levels(key, shape, pieces, -0.22, 0.18) * values
    return jnp.clip(values, min=-limit, max=limit).astype(kind)


def setup_inputs(seed: int = 0) -> dict:
    keys = jax.random.split(jax.random.key(seed), 8)
    return {
        "main_query": scatter_about(keys[0], (QUERIES, HEADS, LATENT), 1.0, 6.0, ((0, 16), (1, 16))),
        "latent_keys": scatter_about(keys[1], (KEYS, LATENT), 1.0, 6.0, ((0, 16),)),
        "head_lse": jnp.clip(4.0 + 4.0 * jax.random.uniform(keys[2], (QUERIES, HEADS), jnp.float32) ** shard_levels(keys[2], (QUERIES, HEADS), ((1, 16),), -0.2, 0.2), 4.0, 8.0),
        "lengths": draw_lengths(jax.random.fold_in(keys[7], 71), 0),
        "index_query": draw_index_query(jax.random.fold_in(keys[7], 71), 0),
        "index_key": draw_index_key(jax.random.fold_in(keys[7], 71), 0),
        "index_weight": draw_index_weight(jax.random.fold_in(keys[7], 71), 0),
    }


main_scale = 192.0 ** -0.5
loss_scale = 64.0
masked_low = -1e30


def reference(main_query, latent_keys, head_lse, lengths, index_query, index_key, index_weight):
    block_keys = math.gcd(KEYS, 512)
    block_total = KEYS // block_keys
    key_pos = jnp.arange(KEYS, dtype=jnp.int32)
    visible = key_pos[None, :] < lengths.astype(jnp.int32)[:, None]
    query_wide = main_query.astype(jnp.float32)

    def mass_block(latent_block):
        scores = jnp.einsum("thd,sd->ths", query_wide, latent_block.astype(jnp.float32), precision=lax.Precision.HIGHEST) * main_scale
        return jnp.sum(jnp.exp(scores - head_lse[:, :, None]), axis=1)

    stacked = lax.map(mass_block, latent_keys.reshape(block_total, block_keys, LATENT))
    row_mass = jnp.moveaxis(stacked, 0, 1).reshape(QUERIES, KEYS)
    row_mass = jnp.where(visible, row_mass, 0.0)
    target = row_mass / jnp.sum(row_mass, axis=1)[:, None]

    index_scale = IDX_DIM ** -0.5
    index_wide = index_query.astype(jnp.float32)
    key_blocks = index_key.reshape(block_total, block_keys, IDX_DIM)

    def block_dots(key_block):
        return jnp.einsum("tjd,sd->tjs", index_wide, key_block.astype(jnp.float32), precision=lax.Precision.HIGHEST)

    def block_logits(key_block):
        return jnp.einsum("tj,tjs->ts", index_weight, jax.nn.relu(block_dots(key_block)), precision=lax.Precision.HIGHEST) * index_scale

    logits = jnp.moveaxis(lax.map(block_logits, key_blocks), 0, 1).reshape(QUERIES, KEYS)
    top = jnp.max(jnp.where(visible, logits, masked_low), axis=1)
    weights_exp = jnp.where(visible, jnp.exp(logits - top[:, None]), 0.0)
    probability = weights_exp / jnp.sum(weights_exp, axis=1)[:, None]
    slopes = loss_scale * (probability - target)
    slope_blocks = slopes.reshape(QUERIES, block_total, block_keys).transpose(1, 0, 2)

    def back_step(query_grad, inputs):
        key_block, slope_block = inputs
        products = block_dots(key_block)
        terms = jnp.where(products > 0, slope_block[:, None, :] * index_weight[:, :, None] * index_scale, 0.0)
        terms = lax.optimization_barrier(terms.astype(jnp.bfloat16)).astype(jnp.float32)
        key_wide = key_block.astype(jnp.float32)
        query_grad = query_grad + jnp.einsum("tjs,sd->tjd", terms, key_wide, precision=lax.Precision.HIGHEST)
        key_grad = jnp.einsum("tjs,tjd->sd", terms, index_wide, precision=lax.Precision.HIGHEST)
        return query_grad, key_grad

    start_grad = jnp.zeros((QUERIES, IDX_HEADS, IDX_DIM), jnp.float32)
    query_grad, key_grads = lax.scan(back_step, start_grad, (key_blocks, slope_blocks))
    return query_grad, key_grads.reshape(KEYS, IDX_DIM)
```

```python
import functools

import jax
import jax.numpy as jnp
from jax import lax
from jax.experimental import pallas as pl
from jax.experimental.pallas import tpu as pltpu
from jax.sharding import PartitionSpec as P

MESH = pl.DeviceIdType.MESH
F32 = jnp.float32
BF16 = jnp.bfloat16

log2e = 1.4426950408889634
main_scale = 192.0 ** (-0.5)
loss_scale = 64.0
masked_low = -1e30

NC = 16
NH = 16
NZ = 8
ROWS = 16
HL = 8
LAT = 576
WIDE = 512
REST = LAT - WIDE
IDXH = 64
DIM = 128
KEYS = 2048
TILE = 256
BIG = 512
HEADS = 128


def slot_l(i):
    return 14 if i == 4 else 2 + (i - 1) * 4


def slot_r(i):
    return 3 + (i - 1) * 4


def kernel(
    mq_hbm, lat_hbm, lse_hbm, len_ref, iq_hbm, ik_hbm, iw_hbm, oq_ref, ok_ref,
    rx, qpack, qext, lse_all, lseb, kt, iqraw, qf, qjm, qt, iw_all, wb, ik, ikt, logits, mass,
    st_send, st_recv, terms, gk_send, gk_recv, gk_own, gq_send, gq_recv, gq_own, fin_send, fin_recv,
    load_sem, q_ssem, q_rsem, l_ssem, l_rsem, i_ssem, i_rsem, w_ssem, w_rsem,
    zl_send, zl_recv, zs_send, zs_recv, sib_send, sib_recv, st_ssem, st_rsem,
    gk_ssem, gk_rsem, gq_ssem, gq_rsem, fin_ssem, fin_rsem,
):
    me_c = lax.axis_index("context")
    me_h = lax.axis_index("heads")
    z = me_c // 2
    core = lax.rem(me_c, 2)
    way = 1 - 2 * core
    sibling = me_c + way

    def ctx_of(step, parity):
        return 2 * lax.rem(z + step + 2 * NZ, NZ) + parity

    next_c = ctx_of(way, core)
    prev_c = ctx_of(-way, core)

    source = {0: me_c, 1: sibling}
    for i in range(1, 5):
        source[slot_l(i)] = ctx_of(-way * i, core)
        source[slot_l(i) + (1 if i == 4 else 2)] = ctx_of(way * i, 1 - core)
    for i in range(1, 4):
        source[slot_r(i)] = ctx_of(way * i, core)
        source[slot_r(i) + 2] = ctx_of(-way * i, 1 - core)

    def plane(o):
        return lax.rem(me_h + o, NH)

    def line(o):
        return lax.rem(me_c + o, NC)

    def remote(src, dst, ssem, rsem, axis, target):
        return pltpu.make_async_remote_copy(
            src_ref=src, dst_ref=dst, send_sem=ssem, recv_sem=rsem, device_id={axis: target}, device_id_type=MESH
        )

    loads = [
        pltpu.make_async_copy(mq_hbm.at[me_h], rx.at[me_h], load_sem.at[0]),
        pltpu.make_async_copy(lse_hbm, lse_all.at[me_h], load_sem.at[1]),
        pltpu.make_async_copy(iq_hbm.at[me_h], iqraw.at[me_h], load_sem.at[2]),
        pltpu.make_async_copy(iw_hbm, iw_all.at[me_h], load_sem.at[3]),
        pltpu.make_async_copy(ik_hbm, ik, load_sem.at[4]),
        pltpu.make_async_copy(lat_hbm, kt.at[pl.ds(0, LAT), :], load_sem.at[5]),
    ]
    for load in loads:
        load.start()

    barrier = pltpu.get_barrier_semaphore()
    for target in (sibling, next_c, prev_c):
        pl.semaphore_signal(barrier, inc=1, device_id={"context": target}, device_id_type=MESH)
    for o in range(1, NH):
        pl.semaphore_signal(barrier, inc=1, device_id={"heads": plane(o)}, device_id_type=MESH)
    kt[LAT:, :] = jnp.zeros((WIDE + DIM - LAT, KEYS), BF16)
    pl.semaphore_wait(barrier, NH + 2)

    def q_copy(o):
        to = plane(o)
        return remote(mq_hbm.at[to], rx.at[me_h], q_ssem.at[o], q_rsem.at[me_h], "heads", to)

    def l_copy(o):
        return remote(lse_hbm, lse_all.at[me_h], l_ssem.at[o], l_rsem.at[me_h], "heads", plane(o))

    def i_copy(o):
        to = plane(o)
        return remote(iq_hbm.at[to], iqraw.at[me_h], i_ssem.at[o], i_rsem.at[me_h], "heads", to)

    def w_copy(o):
        return remote(iw_hbm, iw_all.at[me_h], w_ssem.at[o], w_rsem.at[me_h], "heads", plane(o))

    for copy in (q_copy, l_copy, i_copy, w_copy):
        for o in range(1, NH):
            copy(o).start()

    def arrived(buffer, rsem):
        for o in range(1, NH):
            other = plane(o)
            remote(buffer.at[other], buffer.at[other], rsem.at[other], rsem.at[other], "heads", other).wait_recv()

    loads[0].wait()
    arrived(rx, q_rsem)
    groups = []
    for g in range(8):
        group = rx[2 * g : 2 * g + 2].astype(F32).reshape(ROWS, LAT)
        qpack[0, g] = group[:, :WIDE].astype(BF16)
        groups.append(group[:, WIDE:])
    for g in range(4):
        pair = jnp.concatenate([groups[g], groups[g + 4]], axis=1)
        qpack[0, 8, :, g * DIM : (g + 1) * DIM] = pair.astype(BF16)

    cuts = (pl.ds(0, 4), pl.ds(4, 5))

    def chain(i, part, long):
        source_slot = 0 if i == 1 else (slot_l(i - 1) if long else slot_r(i - 1))
        target_slot = slot_l(i) if long else slot_r(i)
        ssem, rsem = (zl_send, zl_recv) if long else (zs_send, zs_recv)
        return remote(
            qpack.at[source_slot, cuts[part]], qpack.at[target_slot, cuts[part]],
            ssem.at[i - 1, part], rsem.at[i - 1, part], "context", next_c if long else prev_c,
        )

    def to_sibling(slot):
        target = {0: 1, 14: 15}.get(slot, slot + 2)
        index = {0: 0, 14: 7}.get(slot, 1 + (slot - 2) // 4 * 2 + (slot - 2) % 4)
        return remote(qpack.at[slot], qpack.at[target], sib_send.at[index], sib_recv.at[index], "context", sibling)

    for part in range(2):
        chain(1, part, True).start()
        chain(1, part, False).start()
    to_sibling(0).start()

    def advance(i, part):
        chain(i, part, True).wait_recv()
        if i < 4:
            chain(i + 1, part, True).start()
            chain(i, part, False).wait_recv()
            if i < 3:
                chain(i + 1, part, False).start()
        if part == 1:
            to_sibling(slot_l(i)).start()
            if i < 4:
                to_sibling(slot_r(i)).start()

    def widen(first, count):
        for slot in range(first, first + count):
            for g in range(4):
                both = qpack[slot, 8, :, g * DIM : (g + 1) * DIM]
                qext[slot, g] = both
                qext[slot, g + 4] = pltpu.roll(both.astype(F32), REST, axis=1).astype(BF16)

    lane_r = lax.broadcasted_iota(jnp.int32, (HEADS, NC * ROWS), 1)

    def shifts():
        table = lse_all[...].reshape(HEADS, NC * ROWS) * log2e
        for slot in range(16):
            picked = jnp.where(lane_r == source[slot] * ROWS + me_h, table, 0.0)
            lseb[slot] = jnp.broadcast_to(jnp.sum(picked, axis=1, keepdims=True), (HEADS, DIM))

    def piece(first, count, low, high):
        def one_tile(i, carry):
            at = pl.ds(pl.multiple_of(i * BIG, BIG), BIG)
            q_all = jnp.concatenate(
                [
                    qpack[first : first + count, :8].reshape(count * HEADS, WIDE),
                    qext[first : first + count].reshape(count * HEADS, DIM),
                ],
                axis=1,
            )
            score = jnp.dot(q_all, kt[:, at], preferred_element_type=F32)
            shift = lseb[first : first + count].reshape(count * HEADS, DIM)
            shift = jnp.concatenate([shift] * (BIG // DIM), axis=1)
            each = jnp.exp2(score * (main_scale * log2e) - shift)
            for b in range(count):
                row = jnp.sum(each[b * HEADS : (b + 1) * HEADS], axis=0, keepdims=True)
                mass[pl.ds(source[first + b], 1), at] = row
            return carry

        lax.fori_loop(low, high, one_tile, 0)

    loads[4].wait()
    for i in range(KEYS // DIM):
        at = pl.ds(i * DIM, DIM)
        ikt[:, at] = jnp.swapaxes(ik[at, :].astype(F32), 0, 1).astype(BF16)
    loads[1].wait()
    arrived(lse_all, l_rsem)
    shifts()
    loads[2].wait()
    arrived(iqraw, i_rsem)
    loads[3].wait()
    arrived(iw_all, w_rsem)
    qf[...] = iqraw[...].astype(F32)
    index_scale = DIM ** (-0.5)
    row_w = lax.broadcasted_iota(jnp.int32, (NC, ROWS, IDXH), 1)
    weights = jnp.sum(jnp.where(row_w == me_h, iw_all[...], 0.0), axis=1) * index_scale
    for j in range(IDXH):
        qjm[pl.ds(j * ROWS, ROWS), :] = qf[:, j, :].astype(BF16)
        wb[pl.ds(j * ROWS, ROWS), :] = jnp.broadcast_to(weights[:, j : j + 1], (ROWS, DIM))

    advance(1, 0)

    for i in range(IDXH * ROWS // DIM):
        at = pl.ds(i * DIM, DIM)
        qt[:, at] = jnp.swapaxes(qjm[at, :].astype(F32), 0, 1).astype(BF16)

    first_key = me_c * KEYS
    row_of = lax.broadcasted_iota(jnp.int32, (ROWS, BIG), 0)
    lane_of = lax.broadcasted_iota(jnp.int32, (ROWS, BIG), 1)
    limit = jnp.zeros((ROWS, BIG), jnp.int32)
    for c in range(NC):
        limit = jnp.where(row_of == c, len_ref[c * ROWS + me_h], limit)
    limit = limit - first_key - lane_of

    def visible(i):
        return i * BIG < limit

    def logits_tile(i, top):
        at = pl.ds(pl.multiple_of(i * BIG, BIG), BIG)
        k_tile = ikt[:, at]
        total = jnp.zeros((ROWS, BIG), F32)
        for r in range(4):
            rows = pl.ds(r * TILE, TILE)
            dots = jnp.maximum(jnp.dot(qjm[rows, :], k_tile, preferred_element_type=F32), 0.0)
            weight = jnp.concatenate([wb[rows, :]] * (BIG // DIM), axis=1)
            total = total + jnp.sum((dots * weight).reshape(TILE // ROWS, ROWS, BIG), axis=0)
        logits[:, at] = total
        return jnp.maximum(top, jnp.where(visible(i), total, masked_low))

    top = lax.fori_loop(0, KEYS // BIG, logits_tile, jnp.full((ROWS, BIG), masked_low, F32))
    own_top = jnp.max(top, axis=1, keepdims=True)

    def share_tile(i, total):
        at = pl.ds(pl.multiple_of(i * BIG, BIG), BIG)
        return total + jnp.where(visible(i), jnp.exp(logits[:, at] - own_top), 0.0)

    own_share = jnp.sum(
        lax.fori_loop(0, KEYS // BIG, share_tile, jnp.zeros((ROWS, BIG), F32)), axis=1, keepdims=True
    )

    loads[5].wait()
    advance(1, 1)
    to_sibling(0).wait_recv()
    widen(0, 2)
    piece(0, 2, 0, 4)
    for i in range(2, 5):
        advance(i, 0)
        to_sibling(slot_l(i - 1)).wait_recv()
        to_sibling(slot_r(i - 1)).wait_recv()
        widen(slot_l(i - 1), 4)
        piece(slot_l(i - 1), 4, 0, 2)
        advance(i, 1)
        piece(slot_l(i - 1), 4, 2, 4)
    to_sibling(14).wait_recv()
    widen(14, 2)
    piece(14, 2, 0, 4)

    def mass_tile(i, total):
        at = pl.ds(pl.multiple_of(i * BIG, BIG), BIG)
        seen = jnp.where(visible(i), mass[:, at], 0.0)
        mass[:, at] = seen
        return total + seen

    own_total = jnp.sum(
        lax.fori_loop(0, KEYS // BIG, mass_tile, jnp.zeros((ROWS, BIG), F32)), axis=1, keepdims=True
    )

    row_s = lax.broadcasted_iota(jnp.int32, (ROWS, DIM), 0)
    lane_s = lax.broadcasted_iota(jnp.int32, (ROWS, DIM), 1)
    packed = jnp.where(lane_s == row_s, own_top, 0.0)
    packed = jnp.where(lane_s == row_s + ROWS, own_share, packed)
    packed = jnp.where(lane_s == row_s + 2 * ROWS, own_total, packed)
    packed = jnp.sum(packed, axis=0, keepdims=True)
    st_send[...] = packed
    st_recv[me_c] = packed

    def stat_copy(o):
        return remote(st_send, st_recv.at[me_c], st_ssem.at[o], st_rsem.at[me_c], "context", line(o))

    for o in range(1, NC):
        stat_copy(o).start()

    def arrived_line(buffer, rsem):
        for o in range(1, NC):
            other = line(o)
            remote(buffer.at[other], buffer.at[other], rsem.at[other], rsem.at[other], "context", other).wait_recv()

    arrived_line(st_recv, st_rsem)

    stats = jnp.concatenate([st_recv[c] for c in range(NC)], axis=0)
    top_row = jnp.max(stats, axis=0, keepdims=True)
    share_row = jnp.sum(pltpu.roll(stats, DIM - ROWS, axis=1) * jnp.exp(stats - top_row), axis=0, keepdims=True)
    total_row = jnp.sum(pltpu.roll(stats, DIM - 2 * ROWS, axis=1), axis=0, keepdims=True)

    def column_of(row):
        wide = jnp.broadcast_to(row, (ROWS, DIM))
        return jnp.sum(jnp.where(lane_s == row_s, wide, 0.0), axis=1, keepdims=True)

    top_col = column_of(top_row)
    share_col = loss_scale / column_of(share_row)
    total_col = loss_scale / column_of(total_row)

    def slope_tile(i, carry):
        at = pl.ds(pl.multiple_of(i * BIG, BIG), BIG)
        chance = jnp.where(visible(i), jnp.exp(logits[:, at] - top_col), 0.0)
        mass[:, at] = chance * share_col - mass[:, at] * total_col
        return carry

    lax.fori_loop(0, KEYS // BIG, slope_tile, 0)

    def gq_copy(owner):
        return remote(gq_send.at[owner], gq_recv.at[me_c], gq_ssem.at[owner], gq_rsem.at[me_c], "context", owner)

    def query_rows(i, carry):
        chunk = lax.rem(me_c // 4 + 1 + i, 4)
        rows = pl.ds(pl.multiple_of(chunk * TILE, TILE), TILE)
        weight = jnp.concatenate([wb[rows, :]] * (BIG // DIM), axis=1).reshape(TILE // ROWS, ROWS, BIG)

        def term_tile(t, inner):
            at = pl.ds(pl.multiple_of(t * BIG, BIG), BIG)
            dots = jnp.dot(qjm[rows, :], ikt[:, at], preferred_element_type=F32).reshape(TILE // ROWS, ROWS, BIG)
            term = jnp.where(dots > 0, mass[:, at][None] * weight, 0.0)
            terms[rows, at] = term.reshape(TILE, BIG).astype(BF16)
            return inner

        lax.fori_loop(0, KEYS // BIG, term_tile, 0)
        grad = jnp.dot(terms[rows, :], ik[...], preferred_element_type=F32)
        for b in range(4):
            owner = chunk * 4 + b
            part = grad[b * 64 : (b + 1) * 64, :]
            gq_send[owner] = part.astype(BF16)

            @pl.when(owner != me_c)
            def _():
                gq_copy(owner).start()

            @pl.when(owner == me_c)
            def _():
                gq_own[...] = part

        return carry

    lax.fori_loop(0, 4, query_rows, 0)

    def gk_copy(owner):
        return remote(gk_send.at[owner], gk_recv.at[me_h], gk_ssem.at[owner], gk_rsem.at[me_h], "heads", owner)

    def key_tile(i, carry):
        quad = lax.rem(me_h // 4 + 1 + i, 4)
        at = pl.ds(pl.multiple_of(quad * BIG, BIG), BIG)
        grad = jnp.dot(qt[...], terms[:, at], preferred_element_type=F32)
        for b in range(4):
            owner = quad * 4 + b
            part = grad[:, b * DIM : (b + 1) * DIM]
            gk_send[owner] = part.astype(BF16)

            @pl.when(owner != me_h)
            def _():
                gk_copy(owner).start()

            @pl.when(owner == me_h)
            def _():
                gk_own[...] = part

        return carry

    lax.fori_loop(0, 4, key_tile, 0)

    arrived_line(gq_recv, gq_rsem)
    query_sum = gq_own[...]
    for o in range(1, NC):
        query_sum = query_sum + gq_recv[line(o)].astype(F32)
    for j in range(IDXH // NC):
        fin_send[:, j, :] = query_sum[j * ROWS : (j + 1) * ROWS, :]

    def fin_copy(o):
        to = plane(o)
        return remote(fin_send.at[to], fin_recv.at[me_h], fin_ssem.at[o], fin_rsem.at[me_h], "heads", to)

    for o in range(1, NH):
        fin_copy(o).start()
    fin_recv[me_h] = fin_send[me_h]

    arrived(gk_recv, gk_rsem)
    key_sum = gk_own[...]
    for o in range(1, NH):
        key_sum = key_sum + gk_recv[plane(o)].astype(F32)
    ok_ref[...] = jnp.swapaxes(key_sum, 0, 1)

    arrived(fin_recv, fin_rsem)
    oq_ref[...] = fin_recv[...]

    for part in range(2):
        for i in range(1, 5):
            chain(i, part, True).wait_send()
        for i in range(1, 4):
            chain(i, part, False).wait_send()
    for slot in (0, 2, 3, 6, 7, 10, 11, 14):
        to_sibling(slot).wait_send()
    for o in range(1, NC):
        for copy in (q_copy, l_copy, i_copy, w_copy, stat_copy, fin_copy):
            copy(o).wait_send()
        gk_copy(plane(o)).wait_send()
        gq_copy(line(o)).wait_send()


def on_device(main_query, latent_keys, head_lse, lengths, index_query, index_key, index_weight):
    hbm = pl.BlockSpec(memory_space=pl.ANY)
    vmem = pl.BlockSpec(memory_space=pltpu.VMEM)
    smem = pl.BlockSpec(memory_space=pltpu.SMEM)
    dma = pltpu.SemaphoreType.DMA
    return pl.pallas_call(
        kernel,
        out_shape=(
            jax.ShapeDtypeStruct((ROWS, IDXH // NC, DIM), F32),
            jax.ShapeDtypeStruct((KEYS // NH, DIM), F32),
        ),
        in_specs=[hbm, hbm, hbm, smem, hbm, hbm, hbm],
        out_specs=(vmem, vmem),
        scratch_shapes=[
            pltpu.VMEM((NH, HL, LAT), BF16),
            pltpu.VMEM((16, 9, ROWS, WIDE), BF16),
            pltpu.VMEM((16, 8, ROWS, DIM), BF16),
            pltpu.VMEM((NH, HL, NC * ROWS), F32),
            pltpu.VMEM((16, HEADS, DIM), F32),
            pltpu.VMEM((WIDE + DIM, KEYS), BF16),
            pltpu.VMEM((NH, IDXH, DIM), BF16),
            pltpu.VMEM((NH, IDXH, DIM), F32),
            pltpu.VMEM((IDXH * ROWS, DIM), BF16),
            pltpu.VMEM((DIM, IDXH * ROWS), BF16),
            pltpu.VMEM((NH, ROWS, IDXH), F32),
            pltpu.VMEM((IDXH * ROWS, DIM), F32),
            pltpu.VMEM((KEYS, DIM), BF16),
            pltpu.VMEM((DIM, KEYS), BF16),
            pltpu.VMEM((ROWS, KEYS), F32),
            pltpu.VMEM((ROWS, KEYS), F32),
            pltpu.VMEM((1, DIM), F32),
            pltpu.VMEM((NC, 1, DIM), F32),
            pltpu.VMEM((IDXH * ROWS, KEYS), BF16),
            pltpu.VMEM((NH, DIM, DIM), BF16),
            pltpu.VMEM((NH, DIM, DIM), BF16),
            pltpu.VMEM((DIM, DIM), F32),
            pltpu.VMEM((NC, 64, DIM), BF16),
            pltpu.VMEM((NC, 64, DIM), BF16),
            pltpu.VMEM((64, DIM), F32),
            pltpu.VMEM((NH, IDXH // NC, DIM), F32),
            pltpu.VMEM((NH, IDXH // NC, DIM), F32),
            dma((6,)),
            *[dma((16,))] * 8,
            dma((4, 2)),
            dma((4, 2)),
            dma((3, 2)),
            dma((3, 2)),
            dma((8,)),
            dma((8,)),
            *[dma((16,))] * 8,
        ],
        compiler_params=pltpu.CompilerParams(
            collective_id=0, has_side_effects=True, vmem_limit_bytes=56 * 1024 * 1024
        ),
        name="index_grads",
    )(main_query, latent_keys.T, head_lse.T, lengths, index_query, index_key, index_weight)


def solution(mesh):
    placed = (
        P("context", "heads", None),
        P("context", None),
        P(None, "heads"),
        P(),
        P("heads", None, None),
        P("context", None),
        P("heads", None),
    )
    return jax.shard_map(
        on_device,
        mesh=mesh,
        in_specs=placed,
        out_specs=(P("heads", "context", None), P(("context", "heads"), None)),
        check_vma=False,
    )
```

```python
import functools

import jax
import jax.numpy as jnp
from jax import lax
from jax.experimental import pallas as pl
from jax.experimental.pallas import tpu as pltpu
from jax.sharding import PartitionSpec as P

MESH = pl.DeviceIdType.MESH
F32 = jnp.float32
BF16 = jnp.bfloat16

log2e = 1.4426950408889634
main_scale = 192.0 ** (-0.5)
loss_scale = 64.0
masked_low = -1e30

NC = 16
NH = 16
NZ = 8
ROWS = 16
HL = 8
LAT = 576
WIDE = 512
REST = LAT - WIDE
IDXH = 64
DIM = 128
KEYS = 2048
TILE = 256
BIG = 512
HEADS = 128


def slot_l(i):
    return 14 if i == 4 else 2 + (i - 1) * 4


def slot_r(i):
    return 3 + (i - 1) * 4


def kernel(
    mq_hbm, lat_hbm, lse_hbm, len_ref, iq_hbm, ik_hbm, iw_hbm, oq_ref, ok_ref,
    qraw, rx, qpack, qext, lse_all, lseb, kt, iqraw, qf, qjm, qt, iwv, wb, ik, ikt, wm, logits, mass, msend, mrecv,
    st_send, st_recv, terms, gk_send, gk_recv, gk_own, gq_send, gq_recv, gq_own,
    load_sem, q_ssem, q_rsem, l_ssem, l_rsem, m_ssem, m_rsem,
    zl_send, zl_recv, zs_send, zs_recv, sib_send, sib_recv, st_ssem, st_rsem,
    gk_ssem, gk_rsem, gq_ssem, gq_rsem,
):
    me_c = lax.axis_index("context")
    me_h = lax.axis_index("heads")
    z = me_c // 2
    core = lax.rem(me_c, 2)
    way = 1 - 2 * core
    sibling = me_c + way

    def ctx_of(step, parity):
        return 2 * lax.rem(z + step + 2 * NZ, NZ) + parity

    next_c = ctx_of(way, core)
    prev_c = ctx_of(-way, core)

    source = {0: me_c, 1: sibling}
    for i in range(1, 5):
        source[slot_l(i)] = ctx_of(-way * i, core)
        source[slot_l(i) + (1 if i == 4 else 2)] = ctx_of(way * i, 1 - core)
    for i in range(1, 4):
        source[slot_r(i)] = ctx_of(way * i, core)
        source[slot_r(i) + 2] = ctx_of(-way * i, 1 - core)

    def plane(o):
        return lax.rem(me_h + o, NH)

    def line(o):
        return lax.rem(me_c + o, NC)

    def remote(src, dst, ssem, rsem, axis, target):
        return pltpu.make_async_remote_copy(
            src_ref=src, dst_ref=dst, send_sem=ssem, recv_sem=rsem, device_id={axis: target}, device_id_type=MESH
        )

    loads = [
        pltpu.make_async_copy(mq_hbm, qraw, load_sem.at[0]),
        pltpu.make_async_copy(lse_hbm, lse_all.at[me_h], load_sem.at[1]),
        pltpu.make_async_copy(iq_hbm, iqraw, load_sem.at[2]),
        pltpu.make_async_copy(iw_hbm, iwv, load_sem.at[3]),
        pltpu.make_async_copy(ik_hbm, ik, load_sem.at[4]),
        pltpu.make_async_copy(lat_hbm, kt.at[pl.ds(0, LAT), :], load_sem.at[5]),
    ]
    for load in loads:
        load.start()

    barrier = pltpu.get_barrier_semaphore()
    for target in (sibling, next_c, prev_c):
        pl.semaphore_signal(barrier, inc=1, device_id={"context": target}, device_id_type=MESH)
    for o in range(1, NH):
        pl.semaphore_signal(barrier, inc=1, device_id={"heads": plane(o)}, device_id_type=MESH)
    kt[LAT:, :] = jnp.zeros((WIDE + DIM - LAT, KEYS), BF16)
    loads[0].wait()
    rx[me_h] = qraw[me_h]
    loads[4].wait()
    for i in range(KEYS // DIM):
        at = pl.ds(i * DIM, DIM)
        ikt[:, at] = jnp.swapaxes(ik[at, :].astype(F32), 0, 1).astype(BF16)
    loads[2].wait()
    loads[3].wait()
    qf[...] = iqraw[...].astype(F32)
    weights = iwv[...] * DIM ** (-0.5)
    for j in range(IDXH):
        qjm[pl.ds(j * ROWS, ROWS), :] = qf[:, j, :].astype(BF16)
        wb[pl.ds(j * ROWS, ROWS), :] = jnp.broadcast_to(weights[:, j : j + 1], (ROWS, DIM))
    pl.semaphore_wait(barrier, NH + 2)

    def q_copy(o):
        to = plane(o)
        return remote(qraw.at[to], rx.at[me_h], q_ssem.at[o], q_rsem.at[me_h], "heads", to)

    def l_copy(o):
        return remote(lse_hbm, lse_all.at[me_h], l_ssem.at[o], l_rsem.at[me_h], "heads", plane(o))

    for copy in (q_copy, l_copy):
        for o in range(1, NH):
            copy(o).start()

    def arrived(buffer, rsem):
        for o in range(1, NH):
            other = plane(o)
            remote(buffer.at[other], buffer.at[other], rsem.at[other], rsem.at[other], "heads", other).wait_recv()

    first_key = me_c * KEYS
    row_of = lax.broadcasted_iota(jnp.int32, (ROWS, BIG), 0)
    lane_of = lax.broadcasted_iota(jnp.int32, (ROWS, BIG), 1)
    limit = jnp.zeros((ROWS, BIG), jnp.int32)
    for t in range(ROWS):
        limit = jnp.where(row_of == t, len_ref[me_h * ROWS + t], limit)
    limit = limit - first_key - lane_of

    def visible(i):
        return i * BIG < limit

    def logits_tile(i, top):
        at = pl.ds(pl.multiple_of(i * BIG, BIG), BIG)
        k_tile = ikt[:, at]
        total = jnp.zeros((ROWS, BIG), F32)
        for r in range(4):
            rows = pl.ds(r * TILE, TILE)
            dots = jnp.dot(qjm[rows, :], k_tile, preferred_element_type=F32)
            weight = jnp.concatenate([wb[rows, :]] * (BIG // DIM), axis=1)
            masked = jnp.where(dots > 0, weight, 0.0)
            wm[rows, at] = masked
            total = total + jnp.sum((dots * masked).reshape(TILE // ROWS, ROWS, BIG), axis=0)
        logits[:, at] = total
        return jnp.maximum(top, jnp.where(visible(i), total, masked_low))

    top = lax.fori_loop(0, KEYS // BIG, logits_tile, jnp.full((ROWS, BIG), masked_low, F32))
    own_top = jnp.max(top, axis=1, keepdims=True)

    def share_tile(i, total):
        at = pl.ds(pl.multiple_of(i * BIG, BIG), BIG)
        return total + jnp.where(visible(i), jnp.exp(logits[:, at] - own_top), 0.0)

    own_share = jnp.sum(
        lax.fori_loop(0, KEYS // BIG, share_tile, jnp.zeros((ROWS, BIG), F32)), axis=1, keepdims=True
    )

    arrived(rx, q_rsem)
    groups = []
    for g in range(8):
        group = rx[2 * g : 2 * g + 2].astype(F32).reshape(ROWS, LAT)
        qpack[0, g] = group[:, :WIDE].astype(BF16)
        groups.append(group[:, WIDE:])
    for g in range(4):
        pair = jnp.concatenate([groups[g], groups[g + 4]], axis=1)
        qpack[0, 8, :, g * DIM : (g + 1) * DIM] = pair.astype(BF16)

    cuts = (pl.ds(0, 4), pl.ds(4, 5))

    def chain(i, part, long):
        source_slot = 0 if i == 1 else (slot_l(i - 1) if long else slot_r(i - 1))
        target_slot = slot_l(i) if long else slot_r(i)
        ssem, rsem = (zl_send, zl_recv) if long else (zs_send, zs_recv)
        return remote(
            qpack.at[source_slot, cuts[part]], qpack.at[target_slot, cuts[part]],
            ssem.at[i - 1, part], rsem.at[i - 1, part], "context", next_c if long else prev_c,
        )

    def to_sibling(slot):
        target = {0: 1, 14: 15}.get(slot, slot + 2)
        index = {0: 0, 14: 7}.get(slot, 1 + (slot - 2) // 4 * 2 + (slot - 2) % 4)
        return remote(qpack.at[slot], qpack.at[target], sib_send.at[index], sib_recv.at[index], "context", sibling)

    for part in range(2):
        chain(1, part, True).start()
        chain(1, part, False).start()
    to_sibling(0).start()

    def advance(i, part):
        chain(i, part, True).wait_recv()
        if i < 4:
            chain(i + 1, part, True).start()
            chain(i, part, False).wait_recv()
            if i < 3:
                chain(i + 1, part, False).start()
        if part == 1:
            to_sibling(slot_l(i)).start()
            if i < 4:
                to_sibling(slot_r(i)).start()

    def widen(first, count):
        for slot in range(first, first + count):
            for g in range(4):
                both = qpack[slot, 8, :, g * DIM : (g + 1) * DIM]
                qext[slot, g] = both
                qext[slot, g + 4] = pltpu.roll(both.astype(F32), REST, axis=1).astype(BF16)

    def mass_copy(slot):
        to = source[slot]
        return remote(msend.at[to], mrecv.at[me_h], m_ssem.at[slot], m_rsem.at[me_h], "heads", to)

    def deliver(first, count):
        for slot in range(first, first + count):

            @pl.when(source[slot] != me_h)
            def _():
                mass_copy(slot).start()

            @pl.when(source[slot] == me_h)
            def _():
                mrecv[me_h] = msend[me_h]

    lane_r = lax.broadcasted_iota(jnp.int32, (HEADS, NC * ROWS), 1)

    def shifts():
        table = lse_all[...].reshape(HEADS, NC * ROWS) * log2e
        for slot in range(16):
            picked = jnp.where(lane_r == source[slot] * ROWS + me_h, table, 0.0)
            lseb[slot] = jnp.broadcast_to(jnp.sum(picked, axis=1, keepdims=True), (HEADS, DIM))

    def piece(first, count, low, high):
        def one_tile(i, carry):
            at = pl.ds(pl.multiple_of(i * BIG, BIG), BIG)
            q_all = jnp.concatenate(
                [
                    qpack[first : first + count, :8].reshape(count * HEADS, WIDE),
                    qext[first : first + count].reshape(count * HEADS, DIM),
                ],
                axis=1,
            )
            score = jnp.dot(q_all, kt[:, at], preferred_element_type=F32)
            shift = lseb[first : first + count].reshape(count * HEADS, DIM)
            shift = jnp.concatenate([shift] * (BIG // DIM), axis=1)
            each = jnp.exp2(score * (main_scale * log2e) - shift)
            for b in range(count):
                row = jnp.sum(each[b * HEADS : (b + 1) * HEADS], axis=0, keepdims=True)
                msend[source[first + b], :, at] = row
            return carry

        lax.fori_loop(low, high, one_tile, 0)

    def siblings_of(i):
        to_sibling(slot_l(i)).wait_recv()
        to_sibling(slot_r(i)).wait_recv()
        widen(slot_l(i), 4)

    loads[1].wait()
    arrived(lse_all, l_rsem)
    shifts()
    advance(1, 0)
    advance(1, 1)
    loads[5].wait()
    to_sibling(0).wait_recv()
    widen(0, 2)
    piece(0, 2, 0, 4)
    deliver(0, 2)
    advance(2, 0)
    for i in range(IDXH * ROWS // DIM):
        at = pl.ds(i * DIM, DIM)
        qt[:, at] = jnp.swapaxes(qjm[at, :].astype(F32), 0, 1).astype(BF16)
    advance(2, 1)
    siblings_of(1)
    piece(slot_l(1), 4, 0, 3)
    advance(3, 0)
    piece(slot_l(1), 4, 3, 4)
    deliver(slot_l(1), 4)
    advance(3, 1)
    siblings_of(2)
    piece(slot_l(2), 4, 0, 3)
    advance(4, 0)
    piece(slot_l(2), 4, 3, 4)
    deliver(slot_l(2), 4)
    siblings_of(3)
    piece(slot_l(3), 4, 0, 2)
    advance(4, 1)
    piece(slot_l(3), 4, 2, 4)
    deliver(slot_l(3), 4)
    to_sibling(14).wait_recv()
    widen(14, 2)
    piece(14, 2, 0, 4)
    deliver(14, 2)

    arrived(mrecv, m_rsem)

    def mass_tile(i, total):
        at = pl.ds(pl.multiple_of(i * BIG, BIG), BIG)
        seen = jnp.where(visible(i), jnp.concatenate([mrecv[t, :, at] for t in range(ROWS)], axis=0), 0.0)
        mass[:, at] = seen
        return total + seen

    own_total = jnp.sum(
        lax.fori_loop(0, KEYS // BIG, mass_tile, jnp.zeros((ROWS, BIG), F32)), axis=1, keepdims=True
    )

    row_s = lax.broadcasted_iota(jnp.int32, (ROWS, DIM), 0)
    lane_s = lax.broadcasted_iota(jnp.int32, (ROWS, DIM), 1)
    packed = jnp.where(lane_s == row_s, own_top, 0.0)
    packed = jnp.where(lane_s == row_s + ROWS, own_share, packed)
    packed = jnp.where(lane_s == row_s + 2 * ROWS, own_total, packed)
    packed = jnp.sum(packed, axis=0, keepdims=True)
    st_send[...] = packed
    st_recv[me_c] = packed

    def stat_copy(o):
        return remote(st_send, st_recv.at[me_c], st_ssem.at[o], st_rsem.at[me_c], "context", line(o))

    for o in range(1, NC):
        stat_copy(o).start()

    def arrived_line(buffer, rsem):
        for o in range(1, NC):
            other = line(o)
            remote(buffer.at[other], buffer.at[other], rsem.at[other], rsem.at[other], "context", other).wait_recv()

    arrived_line(st_recv, st_rsem)

    stats = jnp.concatenate([st_recv[c] for c in range(NC)], axis=0)
    top_row = jnp.max(stats, axis=0, keepdims=True)
    share_row = jnp.sum(pltpu.roll(stats, DIM - ROWS, axis=1) * jnp.exp(stats - top_row), axis=0, keepdims=True)
    total_row = jnp.sum(pltpu.roll(stats, DIM - 2 * ROWS, axis=1), axis=0, keepdims=True)

    def column_of(row):
        wide = jnp.broadcast_to(row, (ROWS, DIM))
        return jnp.sum(jnp.where(lane_s == row_s, wide, 0.0), axis=1, keepdims=True)

    top_col = column_of(top_row)
    share_col = loss_scale / column_of(share_row)
    total_col = loss_scale / column_of(total_row)

    def slope_tile(i, carry):
        at = pl.ds(pl.multiple_of(i * BIG, BIG), BIG)
        chance = jnp.where(visible(i), jnp.exp(logits[:, at] - top_col), 0.0)
        mass[:, at] = chance * share_col - mass[:, at] * total_col
        return carry

    lax.fori_loop(0, KEYS // BIG, slope_tile, 0)

    def gk_copy(owner):
        return remote(gk_send.at[owner], gk_recv.at[me_h], gk_ssem.at[owner], gk_rsem.at[me_h], "heads", owner)

    def key_tile(i, carry):
        quad = lax.rem(me_h // 4 + 1 + i, 4)
        at = pl.ds(pl.multiple_of(quad * BIG, BIG), BIG)
        slope = mass[:, at][None]
        for r in range(4):
            rows = pl.ds(r * TILE, TILE)
            term = wm[rows, at].reshape(TILE // ROWS, ROWS, BIG) * slope
            terms[rows, at] = term.reshape(TILE, BIG).astype(BF16)
        grad = jnp.dot(qt[...], terms[:, at], preferred_element_type=F32)
        for b in range(4):
            owner = quad * 4 + b
            part = grad[:, b * DIM : (b + 1) * DIM]
            gk_send[owner] = part.astype(BF16)

            @pl.when(owner != me_h)
            def _():
                gk_copy(owner).start()

            @pl.when(owner == me_h)
            def _():
                gk_own[...] = part

        return carry

    lax.fori_loop(0, 4, key_tile, 0)

    def gq_copy(owner):
        return remote(gq_send.at[owner], gq_recv.at[me_c], gq_ssem.at[owner], gq_rsem.at[me_c], "context", owner)

    def query_rows(i, carry):
        chunk = lax.rem(me_c // 2 + 4 + (1 - 2 * lax.rem(i, 2)) * ((i + 1) // 2), 8)
        rows = pl.ds(pl.multiple_of(chunk * DIM, DIM), DIM)
        grad = jnp.dot(terms[rows, :], ik[...], preferred_element_type=F32)
        for b in range(2):
            owner = chunk * 2 + b
            part = grad[b * 64 : (b + 1) * 64, :]
            gq_send[owner] = part.astype(BF16)

            @pl.when(owner != me_c)
            def _():
                gq_copy(owner).start()

            @pl.when(owner == me_c)
            def _():
                gq_own[...] = part

        return carry

    lax.fori_loop(0, 8, query_rows, 0)

    arrived(gk_recv, gk_rsem)
    key_sum = gk_own[...]
    for o in range(1, NH):
        key_sum = key_sum + gk_recv[plane(o)].astype(F32)
    ok_ref[...] = jnp.swapaxes(key_sum, 0, 1)

    arrived_line(gq_recv, gq_rsem)
    query_sum = gq_own[...]
    for o in range(1, NC):
        query_sum = query_sum + gq_recv[line(o)].astype(F32)
    for j in range(IDXH // NC):
        oq_ref[:, j, :] = query_sum[j * ROWS : (j + 1) * ROWS, :]

    for part in range(2):
        for i in range(1, 5):
            chain(i, part, True).wait_send()
        for i in range(1, 4):
            chain(i, part, False).wait_send()
    for slot in (0, 2, 3, 6, 7, 10, 11, 14):
        to_sibling(slot).wait_send()
    for slot in range(16):

        @pl.when(source[slot] != me_h)
        def _():
            mass_copy(slot).wait_send()

    for o in range(1, NC):
        for copy in (q_copy, l_copy, stat_copy):
            copy(o).wait_send()
        gk_copy(plane(o)).wait_send()
        gq_copy(line(o)).wait_send()


def finish(query_ref, key_ref, oq_ref, ok_ref):
    oq_ref[...] = query_ref[...]
    ok_ref[...] = key_ref[...]


def on_device(main_query, latent_keys, head_lse, lengths, index_query, index_key, index_weight):
    hbm = pl.BlockSpec(memory_space=pl.ANY)
    vmem = pl.BlockSpec(memory_space=pltpu.VMEM)
    smem = pl.BlockSpec(memory_space=pltpu.SMEM)
    dma = pltpu.SemaphoreType.DMA
    out_query, out_key = pl.pallas_call(
        kernel,
        out_shape=(
            jax.ShapeDtypeStruct((ROWS, IDXH // NC, DIM), F32),
            jax.ShapeDtypeStruct((KEYS // NH, DIM), F32),
        ),
        in_specs=[hbm, hbm, hbm, smem, hbm, hbm, hbm],
        out_specs=(vmem, vmem),
        scratch_shapes=[
            pltpu.VMEM((ROWS, HL, LAT), BF16),
            pltpu.VMEM((NH, HL, LAT), BF16),
            pltpu.VMEM((16, 9, ROWS, WIDE), BF16),
            pltpu.VMEM((16, 8, ROWS, DIM), BF16),
            pltpu.VMEM((NH, HL, NC * ROWS), F32),
            pltpu.VMEM((16, HEADS, DIM), F32),
            pltpu.VMEM((WIDE + DIM, KEYS), BF16),
            pltpu.VMEM((NH, IDXH, DIM), BF16),
            pltpu.VMEM((NH, IDXH, DIM), F32),
            pltpu.VMEM((IDXH * ROWS, DIM), BF16),
            pltpu.VMEM((DIM, IDXH * ROWS), BF16),
            pltpu.VMEM((ROWS, IDXH), F32),
            pltpu.VMEM((IDXH * ROWS, DIM), F32),
            pltpu.VMEM((KEYS, DIM), BF16),
            pltpu.VMEM((DIM, KEYS), BF16),
            pltpu.VMEM((IDXH * ROWS, KEYS), F32),
            pltpu.VMEM((ROWS, KEYS), F32),
            pltpu.VMEM((ROWS, KEYS), F32),
            pltpu.VMEM((16, 1, KEYS), F32),
            pltpu.VMEM((NH, 1, KEYS), F32),
            pltpu.VMEM((1, DIM), F32),
            pltpu.VMEM((NC, 1, DIM), F32),
            pltpu.VMEM((IDXH * ROWS, KEYS), BF16),
            pltpu.VMEM((NH, DIM, DIM), BF16),
            pltpu.VMEM((NH, DIM, DIM), BF16),
            pltpu.VMEM((DIM, DIM), F32),
            pltpu.VMEM((NC, 64, DIM), BF16),
            pltpu.VMEM((NC, 64, DIM), BF16),
            pltpu.VMEM((64, DIM), F32),
            dma((6,)),
            *[dma((16,))] * 6,
            dma((4, 2)),
            dma((4, 2)),
            dma((3, 2)),
            dma((3, 2)),
            dma((8,)),
            dma((8,)),
            *[dma((16,))] * 6,
        ],
        compiler_params=pltpu.CompilerParams(
            collective_id=0, has_side_effects=True, vmem_limit_bytes=56 * 1024 * 1024
        ),
        name="index_grads",
    )(main_query, latent_keys.T, head_lse.T, lengths, index_query, index_key, index_weight)
    return pl.pallas_call(
        finish,
        out_shape=(
            jax.ShapeDtypeStruct((ROWS, IDXH // NC, DIM), F32),
            jax.ShapeDtypeStruct((KEYS // NH, DIM), F32),
        ),
        in_specs=[vmem, vmem],
        out_specs=(vmem, vmem),
        name="finish",
    )(out_query, out_key)


def solution(mesh):
    placed = (
        P("context", "heads", None),
        P("context", None),
        P(None, "heads"),
        P(),
        P("heads", None, None),
        P("context", None),
        P("heads", None),
    )
    return jax.shard_map(
        on_device,
        mesh=mesh,
        in_specs=placed,
        out_specs=(P("heads", "context", None), P(("context", "heads"), None)),
        check_vma=False,
    )
```

```python
import functools

import jax
import jax.numpy as jnp
from jax import lax
from jax.experimental import pallas as pl
from jax.experimental.pallas import tpu as pltpu
from jax.sharding import PartitionSpec as P

MESH = pl.DeviceIdType.MESH
F32 = jnp.float32
BF16 = jnp.bfloat16

log2e = 1.4426950408889634
main_scale = 192.0 ** (-0.5)
loss_scale = 64.0
masked_low = -1e30

NC = 16
NH = 16
NZ = 8
ROWS = 16
HL = 8
LAT = 576
WIDE = 512
REST = LAT - WIDE
IDXH = 64
DIM = 128
KEYS = 2048
TILE = 256
BIG = 512
HEADS = 128


def slot_l(i):
    return 14 if i == 4 else 2 + (i - 1) * 4


def slot_r(i):
    return 3 + (i - 1) * 4


def kernel(
    mq_hbm, lat_hbm, lse_hbm, len_ref, iq_hbm, ik_hbm, iw_hbm, oq_ref, ok_ref,
    qraw, rx, qpack, qext, lse_all, lseb, kt, iqraw, qf, qjm, qt, iwv, wb, ik, ikt, wm, logits, mass, msend, mrecv,
    st_send, st_recv, terms, gk_send, gk_recv, gk_own, gq_send, gq_recv, gq_own,
    load_sem, q_ssem, q_rsem, l_ssem, l_rsem, m_ssem, m_rsem,
    zl_send, zl_recv, zs_send, zs_recv, zb_send, zb_recv, sib_send, sib_recv, st_ssem, st_rsem,
    gk_ssem, gk_rsem, gq_ssem, gq_rsem,
):
    me_c = lax.axis_index("context")
    me_h = lax.axis_index("heads")
    z = me_c // 2
    core = lax.rem(me_c, 2)
    way = 1 - 2 * core
    sibling = me_c + way

    def ctx_of(step, parity):
        return 2 * lax.rem(z + step + 2 * NZ, NZ) + parity

    next_c = ctx_of(way, core)
    prev_c = ctx_of(-way, core)

    source = {0: me_c, 1: sibling}
    for i in range(1, 5):
        source[slot_l(i)] = ctx_of(-way * i, core)
        source[slot_l(i) + (1 if i == 4 else 2)] = ctx_of(way * i, 1 - core)
    for i in range(1, 4):
        source[slot_r(i)] = ctx_of(way * i, core)
        source[slot_r(i) + 2] = ctx_of(-way * i, 1 - core)

    def plane(o):
        return lax.rem(me_h + o, NH)

    def line(o):
        return lax.rem(me_c + o, NC)

    def remote(src, dst, ssem, rsem, axis, target):
        return pltpu.make_async_remote_copy(
            src_ref=src, dst_ref=dst, send_sem=ssem, recv_sem=rsem, device_id={axis: target}, device_id_type=MESH
        )

    loads = [
        pltpu.make_async_copy(mq_hbm, qraw, load_sem.at[0]),
        pltpu.make_async_copy(lse_hbm, lse_all.at[me_h], load_sem.at[1]),
        pltpu.make_async_copy(iq_hbm, iqraw, load_sem.at[2]),
        pltpu.make_async_copy(iw_hbm, iwv, load_sem.at[3]),
        pltpu.make_async_copy(ik_hbm, ik, load_sem.at[4]),
        pltpu.make_async_copy(lat_hbm, kt.at[pl.ds(0, LAT), :], load_sem.at[5]),
    ]
    for load in loads:
        load.start()

    barrier = pltpu.get_barrier_semaphore()
    for target in (sibling, next_c, prev_c):
        pl.semaphore_signal(barrier, inc=1, device_id={"context": target}, device_id_type=MESH)
    for o in range(1, NH):
        pl.semaphore_signal(barrier, inc=1, device_id={"heads": plane(o)}, device_id_type=MESH)
    kt[LAT:, :] = jnp.zeros((WIDE + DIM - LAT, KEYS), BF16)
    loads[0].wait()
    rx[me_h] = qraw[me_h]
    loads[4].wait()
    for i in range(KEYS // DIM):
        at = pl.ds(i * DIM, DIM)
        ikt[:, at] = jnp.swapaxes(ik[at, :].astype(F32), 0, 1).astype(BF16)
    loads[2].wait()
    loads[3].wait()
    qf[...] = iqraw[...].astype(F32)
    weights = iwv[...] * DIM ** (-0.5)
    for j in range(IDXH):
        qjm[pl.ds(j * ROWS, ROWS), :] = qf[:, j, :].astype(BF16)
        wb[pl.ds(j * ROWS, ROWS), :] = jnp.broadcast_to(weights[:, j : j + 1], (ROWS, DIM))
    pl.semaphore_wait(barrier, NH + 2)

    def q_copy(o):
        to = plane(o)
        return remote(qraw.at[to], rx.at[me_h], q_ssem.at[o], q_rsem.at[me_h], "heads", to)

    def l_copy(o):
        return remote(lse_hbm, lse_all.at[me_h], l_ssem.at[o], l_rsem.at[me_h], "heads", plane(o))

    for copy in (q_copy, l_copy):
        for o in range(1, NH):
            copy(o).start()

    def arrived(buffer, rsem):
        for o in range(1, NH):
            other = plane(o)
            remote(buffer.at[other], buffer.at[other], rsem.at[other], rsem.at[other], "heads", other).wait_recv()

    first_key = me_c * KEYS
    row_of = lax.broadcasted_iota(jnp.int32, (ROWS, BIG), 0)
    lane_of = lax.broadcasted_iota(jnp.int32, (ROWS, BIG), 1)
    limit = jnp.zeros((ROWS, BIG), jnp.int32)
    for t in range(ROWS):
        limit = jnp.where(row_of == t, len_ref[me_h * ROWS + t], limit)
    limit = limit - first_key - lane_of

    def visible(i):
        return i * BIG < limit

    def logits_tile(i, top):
        at = pl.ds(pl.multiple_of(i * BIG, BIG), BIG)
        k_tile = ikt[:, at]
        total = jnp.zeros((ROWS, BIG), F32)
        for r in range(4):
            rows = pl.ds(r * TILE, TILE)
            dots = jnp.dot(qjm[rows, :], k_tile, preferred_element_type=F32)
            weight = jnp.concatenate([wb[rows, :]] * (BIG // DIM), axis=1)
            masked = jnp.where(dots > 0, weight, 0.0)
            wm[rows, at] = masked
            total = total + jnp.sum((dots * masked).reshape(TILE // ROWS, ROWS, BIG), axis=0)
        logits[:, at] = total
        return jnp.maximum(top, jnp.where(visible(i), total, masked_low))

    top = lax.fori_loop(0, KEYS // BIG, logits_tile, jnp.full((ROWS, BIG), masked_low, F32))
    own_top = jnp.max(top, axis=1, keepdims=True)

    def share_tile(i, total):
        at = pl.ds(pl.multiple_of(i * BIG, BIG), BIG)
        return total + jnp.where(visible(i), jnp.exp(logits[:, at] - own_top), 0.0)

    own_share = jnp.sum(
        lax.fori_loop(0, KEYS // BIG, share_tile, jnp.zeros((ROWS, BIG), F32)), axis=1, keepdims=True
    )

    arrived(rx, q_rsem)
    groups = []
    for g in range(8):
        group = rx[2 * g : 2 * g + 2].astype(F32).reshape(ROWS, LAT)
        qpack[0, g] = group[:, :WIDE].astype(BF16)
        groups.append(group[:, WIDE:])
    for g in range(4):
        pair = jnp.concatenate([groups[g], groups[g + 4]], axis=1)
        qpack[0, 8, :, g * DIM : (g + 1) * DIM] = pair.astype(BF16)

    cuts = (pl.ds(0, 3), pl.ds(3, 3), pl.ds(6, 3))
    parts = len(cuts)

    def chain(i, part, long):
        source_slot = 0 if i == 1 else (slot_l(i - 1) if long else slot_r(i - 1))
        target_slot = slot_l(i) if long else slot_r(i)
        ssem, rsem = (zl_send, zl_recv) if long else (zs_send, zs_recv)
        return remote(
            qpack.at[source_slot, cuts[part]], qpack.at[target_slot, cuts[part]],
            ssem.at[i - 1, part], rsem.at[i - 1, part], "context", next_c if long else prev_c,
        )

    def last_hop(part):
        return remote(
            qpack.at[slot_l(3), cuts[part]], qpack.at[15, cuts[part]],
            zb_send.at[part], zb_recv.at[part], "context", ctx_of(way, 1 - core),
        )

    def to_sibling(slot):
        target = 1 if slot == 0 else slot + 2
        index = 0 if slot == 0 else 1 + (slot - 2) // 4 * 2 + (slot - 2) % 4
        return remote(qpack.at[slot], qpack.at[target], sib_send.at[index], sib_recv.at[index], "context", sibling)

    for part in range(parts):
        chain(1, part, True).start()
        chain(1, part, False).start()
    to_sibling(0).start()

    def advance(i):
        for part in range(parts):
            chain(i, part, True).wait_recv()
            chain(i + 1, part, True).start()
            if i == 3:
                last_hop(part).start()
            chain(i, part, False).wait_recv()
            if i < 3:
                chain(i + 1, part, False).start()
        to_sibling(slot_l(i)).start()
        to_sibling(slot_r(i)).start()

    def widen(first, count):
        for slot in range(first, first + count):
            for g in range(4):
                both = qpack[slot, 8, :, g * DIM : (g + 1) * DIM]
                qext[slot, g] = both
                qext[slot, g + 4] = pltpu.roll(both.astype(F32), REST, axis=1).astype(BF16)

    def mass_copy(slot):
        to = source[slot]
        return remote(msend.at[to], mrecv.at[me_h], m_ssem.at[slot], m_rsem.at[me_h], "heads", to)

    def deliver(first, count):
        for slot in range(first, first + count):

            @pl.when(source[slot] != me_h)
            def _():
                mass_copy(slot).start()

            @pl.when(source[slot] == me_h)
            def _():
                mrecv[me_h] = msend[me_h]

    lane_r = lax.broadcasted_iota(jnp.int32, (HEADS, NC * ROWS), 1)

    def shifts():
        table = lse_all[...].reshape(HEADS, NC * ROWS) * log2e
        for slot in range(16):
            picked = jnp.where(lane_r == source[slot] * ROWS + me_h, table, 0.0)
            lseb[slot] = jnp.broadcast_to(jnp.sum(picked, axis=1, keepdims=True), (HEADS, DIM))

    def piece(first, count, low, high):
        def one_tile(i, carry):
            at = pl.ds(pl.multiple_of(i * BIG, BIG), BIG)
            q_all = jnp.concatenate(
                [
                    qpack[first : first + count, :8].reshape(count * HEADS, WIDE),
                    qext[first : first + count].reshape(count * HEADS, DIM),
                ],
                axis=1,
            )
            score = jnp.dot(q_all, kt[:, at], preferred_element_type=F32)
            shift = lseb[first : first + count].reshape(count * HEADS, DIM)
            shift = jnp.concatenate([shift] * (BIG // DIM), axis=1)
            each = jnp.exp2(score * (main_scale * log2e) - shift)
            for b in range(count):
                row = jnp.sum(each[b * HEADS : (b + 1) * HEADS], axis=0, keepdims=True)
                msend[source[first + b], :, at] = row
            return carry

        lax.fori_loop(low, high, one_tile, 0)

    def siblings_of(i):
        to_sibling(slot_l(i)).wait_recv()
        to_sibling(slot_r(i)).wait_recv()
        widen(slot_l(i), 4)

    loads[1].wait()
    arrived(lse_all, l_rsem)
    shifts()
    for i in range(IDXH * ROWS // DIM):
        at = pl.ds(i * DIM, DIM)
        qt[:, at] = jnp.swapaxes(qjm[at, :].astype(F32), 0, 1).astype(BF16)
    advance(1)
    loads[5].wait()
    to_sibling(0).wait_recv()
    widen(0, 2)
    piece(0, 2, 0, 4)
    deliver(0, 2)
    advance(2)
    siblings_of(1)
    piece(slot_l(1), 4, 0, 4)
    deliver(slot_l(1), 4)
    advance(3)
    siblings_of(2)
    piece(slot_l(2), 4, 0, 4)
    deliver(slot_l(2), 4)
    siblings_of(3)
    piece(slot_l(3), 4, 0, 4)
    deliver(slot_l(3), 4)
    for part in range(parts):
        chain(4, part, True).wait_recv()
        last_hop(part).wait_recv()
    widen(14, 2)
    piece(14, 2, 0, 4)
    deliver(14, 2)

    arrived(mrecv, m_rsem)

    def mass_tile(i, total):
        at = pl.ds(pl.multiple_of(i * BIG, BIG), BIG)
        seen = jnp.where(visible(i), jnp.concatenate([mrecv[t, :, at] for t in range(ROWS)], axis=0), 0.0)
        mass[:, at] = seen
        return total + seen

    own_total = jnp.sum(
        lax.fori_loop(0, KEYS // BIG, mass_tile, jnp.zeros((ROWS, BIG), F32)), axis=1, keepdims=True
    )

    row_s = lax.broadcasted_iota(jnp.int32, (ROWS, DIM), 0)
    lane_s = lax.broadcasted_iota(jnp.int32, (ROWS, DIM), 1)
    packed = jnp.where(lane_s == row_s, own_top, 0.0)
    packed = jnp.where(lane_s == row_s + ROWS, own_share, packed)
    packed = jnp.where(lane_s == row_s + 2 * ROWS, own_total, packed)
    packed = jnp.sum(packed, axis=0, keepdims=True)
    st_send[...] = packed
    st_recv[me_c] = packed

    def stat_copy(o):
        return remote(st_send, st_recv.at[me_c], st_ssem.at[o], st_rsem.at[me_c], "context", line(o))

    for o in range(1, NC):
        stat_copy(o).start()

    def arrived_line(buffer, rsem):
        for o in range(1, NC):
            other = line(o)
            remote(buffer.at[other], buffer.at[other], rsem.at[other], rsem.at[other], "context", other).wait_recv()

    arrived_line(st_recv, st_rsem)

    stats = jnp.concatenate([st_recv[c] for c in range(NC)], axis=0)
    top_row = jnp.max(stats, axis=0, keepdims=True)
    share_row = jnp.sum(pltpu.roll(stats, DIM - ROWS, axis=1) * jnp.exp(stats - top_row), axis=0, keepdims=True)
    total_row = jnp.sum(pltpu.roll(stats, DIM - 2 * ROWS, axis=1), axis=0, keepdims=True)

    def column_of(row):
        wide = jnp.broadcast_to(row, (ROWS, DIM))
        return jnp.sum(jnp.where(lane_s == row_s, wide, 0.0), axis=1, keepdims=True)

    top_col = column_of(top_row)
    share_col = loss_scale / column_of(share_row)
    total_col = loss_scale / column_of(total_row)

    def slope_tile(i, carry):
        at = pl.ds(pl.multiple_of(i * BIG, BIG), BIG)
        chance = jnp.where(visible(i), jnp.exp(logits[:, at] - top_col), 0.0)
        mass[:, at] = chance * share_col - mass[:, at] * total_col
        return carry

    lax.fori_loop(0, KEYS // BIG, slope_tile, 0)

    def term_tile(i, carry):
        at = pl.ds(pl.multiple_of(i * BIG, BIG), BIG)
        slope = mass[:, at][None]
        for r in range(4):
            rows = pl.ds(r * TILE, TILE)
            term = wm[rows, at].reshape(TILE // ROWS, ROWS, BIG) * slope
            terms[rows, at] = term.reshape(TILE, BIG).astype(BF16)
        return carry

    lax.fori_loop(0, KEYS // BIG, term_tile, 0)

    def gq_copy(owner):
        return remote(gq_send.at[owner], gq_recv.at[me_c], gq_ssem.at[owner], gq_rsem.at[me_c], "context", owner)

    def gk_copy(owner):
        return remote(gk_send.at[owner], gk_recv.at[me_h], gk_ssem.at[owner], gk_rsem.at[me_h], "heads", owner)

    def both_grads(i, carry):
        chunk = lax.rem(me_c // 4 + 2 + (1 - 2 * lax.rem(i, 2)) * ((i + 1) // 2), 4)
        rows = pl.ds(pl.multiple_of(chunk * TILE, TILE), TILE)
        grad = jnp.dot(terms[rows, :], ik[...], preferred_element_type=F32)
        for b in range(4):
            owner = chunk * 4 + b
            part = grad[b * 64 : (b + 1) * 64, :]
            gq_send[owner] = part.astype(BF16)

            @pl.when(owner != me_c)
            def _():
                gq_copy(owner).start()

            @pl.when(owner == me_c)
            def _():
                gq_own[...] = part

        quad = lax.rem(me_h // 4 + 2 + (1 - 2 * lax.rem(i, 2)) * ((i + 1) // 2), 4)
        at = pl.ds(pl.multiple_of(quad * BIG, BIG), BIG)
        grad = jnp.dot(qt[...], terms[:, at], preferred_element_type=F32)
        for b in range(4):
            owner = quad * 4 + b
            part = grad[:, b * DIM : (b + 1) * DIM]
            gk_send[owner] = part.astype(BF16)

            @pl.when(owner != me_h)
            def _():
                gk_copy(owner).start()

            @pl.when(owner == me_h)
            def _():
                gk_own[...] = part

        return carry

    lax.fori_loop(0, 4, both_grads, 0)

    for part in range(parts):
        last_hop(part).wait_send()
        for i in range(1, 5):
            chain(i, part, True).wait_send()
        for i in range(1, 4):
            chain(i, part, False).wait_send()
    for slot in (0, 2, 3, 6, 7, 10, 11):
        to_sibling(slot).wait_send()
    for slot in range(16):

        @pl.when(source[slot] != me_h)
        def _():
            mass_copy(slot).wait_send()

    for o in range(1, NC):
        for copy in (q_copy, l_copy, stat_copy):
            copy(o).wait_send()

    arrived(gk_recv, gk_rsem)
    key_sum = gk_own[...]
    for o in range(1, NH):
        key_sum = key_sum + gk_recv[plane(o)].astype(F32)
    ok_ref[...] = jnp.swapaxes(key_sum, 0, 1)

    arrived_line(gq_recv, gq_rsem)
    query_sum = gq_own[...]
    for o in range(1, NC):
        query_sum = query_sum + gq_recv[line(o)].astype(F32)
    for j in range(IDXH // NC):
        oq_ref[:, j, :] = query_sum[j * ROWS : (j + 1) * ROWS, :]

    for o in range(1, NC):
        gk_copy(plane(o)).wait_send()
        gq_copy(line(o)).wait_send()


def finish(query_ref, key_ref, oq_ref, ok_ref):
    oq_ref[...] = query_ref[...]
    ok_ref[...] = key_ref[...]


def on_device(main_query, latent_keys, head_lse, lengths, index_query, index_key, index_weight):
    hbm = pl.BlockSpec(memory_space=pl.ANY)
    vmem = pl.BlockSpec(memory_space=pltpu.VMEM)
    smem = pl.BlockSpec(memory_space=pltpu.SMEM)
    dma = pltpu.SemaphoreType.DMA
    out_query, out_key = pl.pallas_call(
        kernel,
        out_shape=(
            jax.ShapeDtypeStruct((ROWS, IDXH // NC, DIM), F32),
            jax.ShapeDtypeStruct((KEYS // NH, DIM), F32),
        ),
        in_specs=[hbm, hbm, hbm, smem, hbm, hbm, hbm],
        out_specs=(vmem, vmem),
        scratch_shapes=[
            pltpu.VMEM((ROWS, HL, LAT), BF16),
            pltpu.VMEM((NH, HL, LAT), BF16),
            pltpu.VMEM((16, 9, ROWS, WIDE), BF16),
            pltpu.VMEM((16, 8, ROWS, DIM), BF16),
            pltpu.VMEM((NH, HL, NC * ROWS), F32),
            pltpu.VMEM((16, HEADS, DIM), F32),
            pltpu.VMEM((WIDE + DIM, KEYS), BF16),
            pltpu.VMEM((NH, IDXH, DIM), BF16),
            pltpu.VMEM((NH, IDXH, DIM), F32),
            pltpu.VMEM((IDXH * ROWS, DIM), BF16),
            pltpu.VMEM((DIM, IDXH * ROWS), BF16),
            pltpu.VMEM((ROWS, IDXH), F32),
            pltpu.VMEM((IDXH * ROWS, DIM), F32),
            pltpu.VMEM((KEYS, DIM), BF16),
            pltpu.VMEM((DIM, KEYS), BF16),
            pltpu.VMEM((IDXH * ROWS, KEYS), F32),
            pltpu.VMEM((ROWS, KEYS), F32),
            pltpu.VMEM((ROWS, KEYS), F32),
            pltpu.VMEM((16, 1, KEYS), F32),
            pltpu.VMEM((NH, 1, KEYS), F32),
            pltpu.VMEM((1, DIM), F32),
            pltpu.VMEM((NC, 1, DIM), F32),
            pltpu.VMEM((IDXH * ROWS, KEYS), BF16),
            pltpu.VMEM((NH, DIM, DIM), BF16),
            pltpu.VMEM((NH, DIM, DIM), BF16),
            pltpu.VMEM((DIM, DIM), F32),
            pltpu.VMEM((NC, 64, DIM), BF16),
            pltpu.VMEM((NC, 64, DIM), BF16),
            pltpu.VMEM((64, DIM), F32),
            dma((6,)),
            *[dma((16,))] * 6,
            dma((4, 3)),
            dma((4, 3)),
            dma((3, 3)),
            dma((3, 3)),
            dma((3,)),
            dma((3,)),
            dma((8,)),
            dma((8,)),
            *[dma((16,))] * 6,
        ],
        compiler_params=pltpu.CompilerParams(
            collective_id=0, has_side_effects=True, vmem_limit_bytes=56 * 1024 * 1024
        ),
        name="index_grads",
    )(main_query, latent_keys.T, head_lse.T, lengths, index_query, index_key, index_weight)
    return pl.pallas_call(
        finish,
        out_shape=(
            jax.ShapeDtypeStruct((ROWS, IDXH // NC, DIM), F32),
            jax.ShapeDtypeStruct((KEYS // NH, DIM), F32),
        ),
        in_specs=[vmem, vmem],
        out_specs=(vmem, vmem),
        name="finish",
    )(out_query, out_key)


def solution(mesh):
    placed = (
        P("context", "heads", None),
        P("context", None),
        P(None, "heads"),
        P(),
        P("heads", None, None),
        P("context", None),
        P("heads", None),
    )
    return jax.shard_map(
        on_device,
        mesh=mesh,
        in_specs=placed,
        out_specs=(P("heads", "context", None), P(("context", "heads"), None)),
        check_vma=False,
    )
```

```python
import functools

import jax
import jax.numpy as jnp
from jax import lax
from jax.experimental import pallas as pl
from jax.experimental.pallas import tpu as pltpu
from jax.sharding import PartitionSpec as P

MESH = pl.DeviceIdType.MESH
F32 = jnp.float32
BF16 = jnp.bfloat16

log2e = 1.4426950408889634
main_scale = 192.0 ** (-0.5)
loss_scale = 64.0
masked_low = -1e30

NC = 16
NH = 16
NZ = 8
ROWS = 16
HL = 8
LAT = 576
WIDE = 512
REST = LAT - WIDE
IDXH = 64
DIM = 128
KEYS = 2048
TILE = 256
BIG = 512
HEADS = 128


def slot_l(i):
    return 14 if i == 4 else 2 + (i - 1) * 4


def slot_r(i):
    return 3 + (i - 1) * 4


def kernel(
    mq_hbm, lat_hbm, lse_hbm, len_ref, iq_hbm, ik_hbm, iw_hbm, oq_ref, ok_ref,
    qraw, rx, qpack, qext, lse_all, lseb, kt, iqraw, qf, qjm, qt, iwv, wb, ik, ikt, wm, logits, mass, msend, mrecv,
    st_send, st_recv, terms, gk_send, gk_recv, gk_own, gq_send, gq_recv, gq_own,
    load_sem, q_ssem, q_rsem, l_ssem, l_rsem, m_ssem, m_rsem,
    zl_send, zl_recv, zs_send, zs_recv, zb_send, zb_recv, sib_send, sib_recv, st_ssem, st_rsem,
    gk_ssem, gk_rsem, gq_ssem, gq_rsem,
):
    me_c = lax.axis_index("context")
    me_h = lax.axis_index("heads")
    z = me_c // 2
    core = lax.rem(me_c, 2)
    way = 1 - 2 * core
    sibling = me_c + way

    def ctx_of(step, parity):
        return 2 * lax.rem(z + step + 2 * NZ, NZ) + parity

    next_c = ctx_of(way, core)
    prev_c = ctx_of(-way, core)

    source = {0: me_c, 1: sibling}
    for i in range(1, 5):
        source[slot_l(i)] = ctx_of(-way * i, core)
        source[slot_l(i) + (1 if i == 4 else 2)] = ctx_of(way * i, 1 - core)
    for i in range(1, 4):
        source[slot_r(i)] = ctx_of(way * i, core)
        source[slot_r(i) + 2] = ctx_of(-way * i, 1 - core)

    def plane(o):
        return lax.rem(me_h + o, NH)

    def line(o):
        return lax.rem(me_c + o, NC)

    def remote(src, dst, ssem, rsem, axis, target):
        return pltpu.make_async_remote_copy(
            src_ref=src, dst_ref=dst, send_sem=ssem, recv_sem=rsem, device_id={axis: target}, device_id_type=MESH
        )

    loads = [
        pltpu.make_async_copy(mq_hbm, qraw, load_sem.at[0]),
        pltpu.make_async_copy(lse_hbm, lse_all.at[me_h], load_sem.at[1]),
        pltpu.make_async_copy(iq_hbm, iqraw, load_sem.at[2]),
        pltpu.make_async_copy(iw_hbm, iwv, load_sem.at[3]),
        pltpu.make_async_copy(ik_hbm, ik, load_sem.at[4]),
        pltpu.make_async_copy(lat_hbm, kt.at[pl.ds(0, LAT), :], load_sem.at[5]),
    ]
    for load in loads:
        load.start()

    barrier = pltpu.get_barrier_semaphore()
    for target in (sibling, next_c, prev_c):
        pl.semaphore_signal(barrier, inc=1, device_id={"context": target}, device_id_type=MESH)
    for o in range(1, NH):
        pl.semaphore_signal(barrier, inc=1, device_id={"heads": plane(o)}, device_id_type=MESH)
    kt[LAT:, :] = jnp.zeros((WIDE + DIM - LAT, KEYS), BF16)
    loads[0].wait()
    rx[me_h] = qraw[me_h]
    loads[4].wait()
    for i in range(KEYS // DIM):
        at = pl.ds(i * DIM, DIM)
        ikt[:, at] = jnp.swapaxes(ik[at, :].astype(F32), 0, 1).astype(BF16)
    loads[2].wait()
    loads[3].wait()
    qf[...] = iqraw[...].astype(F32)
    weights = iwv[...] * DIM ** (-0.5)
    for j in range(IDXH):
        qjm[pl.ds(j * ROWS, ROWS), :] = qf[:, j, :].astype(BF16)
        wb[pl.ds(j * ROWS, ROWS), :] = jnp.broadcast_to(weights[:, j : j + 1], (ROWS, DIM))
    pl.semaphore_wait(barrier, NH + 2)

    def q_copy(o):
        to = plane(o)
        return remote(qraw.at[to], rx.at[me_h], q_ssem.at[o], q_rsem.at[me_h], "heads", to)

    def l_copy(o):
        return remote(lse_hbm, lse_all.at[me_h], l_ssem.at[o], l_rsem.at[me_h], "heads", plane(o))

    for o in range(1, NH):
        q_copy(o).start()

    def arrived(buffer, rsem):
        for o in range(1, NH):
            other = plane(o)
            remote(buffer.at[other], buffer.at[other], rsem.at[other], rsem.at[other], "heads", other).wait_recv()

    first_key = me_c * KEYS
    row_of = lax.broadcasted_iota(jnp.int32, (ROWS, BIG), 0)
    lane_of = lax.broadcasted_iota(jnp.int32, (ROWS, BIG), 1)
    limit = jnp.zeros((ROWS, BIG), jnp.int32)
    for t in range(ROWS):
        limit = jnp.where(row_of == t, len_ref[me_h * ROWS + t], limit)
    limit = limit - first_key - lane_of

    def visible(i):
        return i * BIG < limit

    def logits_tile(i, top):
        at = pl.ds(pl.multiple_of(i * BIG, BIG), BIG)
        k_tile = ikt[:, at]
        total = jnp.zeros((ROWS, BIG), F32)
        for r in range(4):
            rows = pl.ds(r * TILE, TILE)
            dots = jnp.dot(qjm[rows, :], k_tile, preferred_element_type=F32)
            weight = jnp.concatenate([wb[rows, :]] * (BIG // DIM), axis=1)
            masked = jnp.where(dots > 0, weight, 0.0)
            wm[rows, at] = masked
            total = total + jnp.sum((dots * masked).reshape(TILE // ROWS, ROWS, BIG), axis=0)
        logits[:, at] = total
        return jnp.maximum(top, jnp.where(visible(i), total, masked_low))

    top = lax.fori_loop(0, KEYS // BIG, logits_tile, jnp.full((ROWS, BIG), masked_low, F32))
    own_top = jnp.max(top, axis=1, keepdims=True)

    def share_tile(i, total):
        at = pl.ds(pl.multiple_of(i * BIG, BIG), BIG)
        return total + jnp.where(visible(i), jnp.exp(logits[:, at] - own_top), 0.0)

    own_share = jnp.sum(
        lax.fori_loop(0, KEYS // BIG, share_tile, jnp.zeros((ROWS, BIG), F32)), axis=1, keepdims=True
    )

    cuts = (pl.ds(0, 3), pl.ds(3, 3), pl.ds(6, 3))
    parts = len(cuts)

    def chain(i, part, long):
        source_slot = 0 if i == 1 else (slot_l(i - 1) if long else slot_r(i - 1))
        target_slot = slot_l(i) if long else slot_r(i)
        ssem, rsem = (zl_send, zl_recv) if long else (zs_send, zs_recv)
        return remote(
            qpack.at[source_slot, cuts[part]], qpack.at[target_slot, cuts[part]],
            ssem.at[i - 1, part], rsem.at[i - 1, part], "context", next_c if long else prev_c,
        )

    def last_hop(part):
        return remote(
            qpack.at[slot_l(3), cuts[part]], qpack.at[15, cuts[part]],
            zb_send.at[part], zb_recv.at[part], "context", ctx_of(way, 1 - core),
        )

    def to_sibling(slot):
        target = 1 if slot == 0 else slot + 2
        index = 0 if slot == 0 else 1 + (slot - 2) // 4 * 2 + (slot - 2) % 4
        return remote(qpack.at[slot], qpack.at[target], sib_send.at[index], sib_recv.at[index], "context", sibling)

    arrived(rx, q_rsem)
    groups = []
    for part in range(parts):
        for g in range(3 * part, min(3 * part + 3, 8)):
            group = rx[2 * g : 2 * g + 2].astype(F32).reshape(ROWS, LAT)
            qpack[0, g] = group[:, :WIDE].astype(BF16)
            groups.append(group[:, WIDE:])
        if part == parts - 1:
            for g in range(4):
                pair = jnp.concatenate([groups[g], groups[g + 4]], axis=1)
                qpack[0, 8, :, g * DIM : (g + 1) * DIM] = pair.astype(BF16)
        chain(1, part, True).start()
        chain(1, part, False).start()
    to_sibling(0).start()
    for o in range(1, NH):
        l_copy(o).start()

    def advance(i):
        for part in range(parts):
            chain(i, part, True).wait_recv()
            chain(i + 1, part, True).start()
            if i == 3:
                last_hop(part).start()
            chain(i, part, False).wait_recv()
            if i < 3:
                chain(i + 1, part, False).start()
        to_sibling(slot_l(i)).start()
        to_sibling(slot_r(i)).start()

    def widen(first, count):
        for slot in range(first, first + count):
            for g in range(4):
                both = qpack[slot, 8, :, g * DIM : (g + 1) * DIM]
                qext[slot, g] = both
                qext[slot, g + 4] = pltpu.roll(both.astype(F32), REST, axis=1).astype(BF16)

    def mass_copy(slot):
        to = source[slot]
        return remote(msend.at[to], mrecv.at[me_h], m_ssem.at[slot], m_rsem.at[me_h], "heads", to)

    def deliver(first, count):
        for slot in range(first, first + count):

            @pl.when(source[slot] != me_h)
            def _():
                mass_copy(slot).start()

            @pl.when(source[slot] == me_h)
            def _():
                mrecv[me_h] = msend[me_h]

    lane_r = lax.broadcasted_iota(jnp.int32, (HEADS, NC * ROWS), 1)

    def shifts():
        table = lse_all[...].reshape(HEADS, NC * ROWS) * log2e
        for slot in range(16):
            picked = jnp.where(lane_r == source[slot] * ROWS + me_h, table, 0.0)
            lseb[slot] = jnp.broadcast_to(jnp.sum(picked, axis=1, keepdims=True), (HEADS, DIM))

    def piece(first, count, low, high):
        def one_tile(i, carry):
            at = pl.ds(pl.multiple_of(i * BIG, BIG), BIG)
            q_all = jnp.concatenate(
                [
                    qpack[first : first + count, :8].reshape(count * HEADS, WIDE),
                    qext[first : first + count].reshape(count * HEADS, DIM),
                ],
                axis=1,
            )
            score = jnp.dot(q_all, kt[:, at], preferred_element_type=F32)
            shift = lseb[first : first + count].reshape(count * HEADS, DIM)
            shift = jnp.concatenate([shift] * (BIG // DIM), axis=1)
            each = jnp.exp2(score * (main_scale * log2e) - shift)
            for b in range(count):
                row = jnp.sum(each[b * HEADS : (b + 1) * HEADS], axis=0, keepdims=True)
                msend[source[first + b], :, at] = row
            return carry

        lax.fori_loop(low, high, one_tile, 0)

    def siblings_of(i):
        to_sibling(slot_l(i)).wait_recv()
        to_sibling(slot_r(i)).wait_recv()
        widen(slot_l(i), 4)

    for i in range(IDXH * ROWS // DIM):
        at = pl.ds(i * DIM, DIM)
        qt[:, at] = jnp.swapaxes(qjm[at, :].astype(F32), 0, 1).astype(BF16)
    advance(1)
    loads[1].wait()
    arrived(lse_all, l_rsem)
    shifts()
    loads[5].wait()
    to_sibling(0).wait_recv()
    widen(0, 2)
    piece(0, 2, 0, 4)
    deliver(0, 2)
    advance(2)
    siblings_of(1)
    piece(slot_l(1), 4, 0, 4)
    deliver(slot_l(1), 4)
    advance(3)
    siblings_of(2)
    piece(slot_l(2), 4, 0, 4)
    deliver(slot_l(2), 4)
    siblings_of(3)
    piece(slot_l(3), 4, 0, 4)
    deliver(slot_l(3), 4)
    for part in range(parts):
        chain(4, part, True).wait_recv()
        last_hop(part).wait_recv()
    widen(14, 2)
    piece(14, 2, 0, 4)
    deliver(14, 2)

    arrived(mrecv, m_rsem)

    def mass_tile(i, total):
        at = pl.ds(pl.multiple_of(i * BIG, BIG), BIG)
        seen = jnp.where(visible(i), jnp.concatenate([mrecv[t, :, at] for t in range(ROWS)], axis=0), 0.0)
        mass[:, at] = seen
        return total + seen

    own_total = jnp.sum(
        lax.fori_loop(0, KEYS // BIG, mass_tile, jnp.zeros((ROWS, BIG), F32)), axis=1, keepdims=True
    )

    row_s = lax.broadcasted_iota(jnp.int32, (ROWS, DIM), 0)
    lane_s = lax.broadcasted_iota(jnp.int32, (ROWS, DIM), 1)
    packed = jnp.where(lane_s == row_s, own_top, 0.0)
    packed = jnp.where(lane_s == row_s + ROWS, own_share, packed)
    packed = jnp.where(lane_s == row_s + 2 * ROWS, own_total, packed)
    packed = jnp.sum(packed, axis=0, keepdims=True)
    st_send[...] = packed
    st_recv[me_c] = packed

    def stat_copy(o):
        return remote(st_send, st_recv.at[me_c], st_ssem.at[o], st_rsem.at[me_c], "context", line(o))

    for o in range(1, NC):
        stat_copy(o).start()

    def arrived_line(buffer, rsem):
        for o in range(1, NC):
            other = line(o)
            remote(buffer.at[other], buffer.at[other], rsem.at[other], rsem.at[other], "context", other).wait_recv()

    arrived_line(st_recv, st_rsem)

    stats = jnp.concatenate([st_recv[c] for c in range(NC)], axis=0)
    top_row = jnp.max(stats, axis=0, keepdims=True)
    share_row = jnp.sum(pltpu.roll(stats, DIM - ROWS, axis=1) * jnp.exp(stats - top_row), axis=0, keepdims=True)
    total_row = jnp.sum(pltpu.roll(stats, DIM - 2 * ROWS, axis=1), axis=0, keepdims=True)

    def column_of(row):
        wide = jnp.broadcast_to(row, (ROWS, DIM))
        return jnp.sum(jnp.where(lane_s == row_s, wide, 0.0), axis=1, keepdims=True)

    top_col = column_of(top_row)
    share_col = loss_scale / column_of(share_row)
    total_col = loss_scale / column_of(total_row)

    def slope_tile(i, carry):
        at = pl.ds(pl.multiple_of(i * BIG, BIG), BIG)
        chance = jnp.where(visible(i), jnp.exp(logits[:, at] - top_col), 0.0)
        mass[:, at] = chance * share_col - mass[:, at] * total_col
        return carry

    lax.fori_loop(0, KEYS // BIG, slope_tile, 0)

    def term_tile(i, carry):
        at = pl.ds(pl.multiple_of(i * BIG, BIG), BIG)
        slope = mass[:, at][None]
        for r in range(4):
            rows = pl.ds(r * TILE, TILE)
            term = wm[rows, at].reshape(TILE // ROWS, ROWS, BIG) * slope
            terms[rows, at] = term.reshape(TILE, BIG).astype(BF16)
        return carry

    lax.fori_loop(0, KEYS // BIG, term_tile, 0)

    def gq_copy(owner):
        return remote(gq_send.at[owner], gq_recv.at[me_c], gq_ssem.at[owner], gq_rsem.at[me_c], "context", owner)

    def gk_copy(owner):
        return remote(gk_send.at[owner], gk_recv.at[me_h], gk_ssem.at[owner], gk_rsem.at[me_h], "heads", owner)

    def both_grads(i, carry):
        quad = lax.rem(me_h // 4 + 2 + (1 - 2 * lax.rem(i, 2)) * ((i + 1) // 2), 4)
        at = pl.ds(pl.multiple_of(quad * BIG, BIG), BIG)
        grad = jnp.dot(qt[...], terms[:, at], preferred_element_type=F32)
        for b in range(4):
            owner = quad * 4 + b
            part = grad[:, b * DIM : (b + 1) * DIM]
            gk_send[owner] = part.astype(BF16)

            @pl.when(owner != me_h)
            def _():
                gk_copy(owner).start()

            @pl.when(owner == me_h)
            def _():
                gk_own[...] = part

        chunk = lax.rem(me_c // 4 + 2 + (1 - 2 * lax.rem(i, 2)) * ((i + 1) // 2), 4)
        rows = pl.ds(pl.multiple_of(chunk * TILE, TILE), TILE)
        grad = jnp.dot(terms[rows, :], ik[...], preferred_element_type=F32)
        for b in range(4):
            owner = chunk * 4 + b
            part = grad[b * 64 : (b + 1) * 64, :]
            gq_send[owner] = part.astype(BF16)

            @pl.when(owner != me_c)
            def _():
                gq_copy(owner).start()

            @pl.when(owner == me_c)
            def _():
                gq_own[...] = part

        return carry

    lax.fori_loop(0, 4, both_grads, 0)

    for part in range(parts):
        last_hop(part).wait_send()
        for i in range(1, 5):
            chain(i, part, True).wait_send()
        for i in range(1, 4):
            chain(i, part, False).wait_send()
    for slot in (0, 2, 3, 6, 7, 10, 11):
        to_sibling(slot).wait_send()
    for slot in range(16):

        @pl.when(source[slot] != me_h)
        def _():
            mass_copy(slot).wait_send()

    for o in range(1, NC):
        for copy in (q_copy, l_copy, stat_copy):
            copy(o).wait_send()

    arrived(gk_recv, gk_rsem)
    key_sum = gk_own[...]
    for o in range(1, NH):
        key_sum = key_sum + gk_recv[plane(o)].astype(F32)
    ok_ref[...] = jnp.swapaxes(key_sum, 0, 1)

    arrived_line(gq_recv, gq_rsem)
    query_sum = gq_own[...]
    for o in range(1, NC):
        query_sum = query_sum + gq_recv[line(o)].astype(F32)
    for j in range(IDXH // NC):
        oq_ref[:, j, :] = query_sum[j * ROWS : (j + 1) * ROWS, :]

    for o in range(1, NC):
        gk_copy(plane(o)).wait_send()
        gq_copy(line(o)).wait_send()


def finish(query_ref, key_ref, oq_ref, ok_ref):
    oq_ref[...] = query_ref[...]
    ok_ref[...] = key_ref[...]


def on_device(main_query, latent_keys, head_lse, lengths, index_query, index_key, index_weight):
    hbm = pl.BlockSpec(memory_space=pl.ANY)
    vmem = pl.BlockSpec(memory_space=pltpu.VMEM)
    smem = pl.BlockSpec(memory_space=pltpu.SMEM)
    dma = pltpu.SemaphoreType.DMA
    out_query, out_key = pl.pallas_call(
        kernel,
        out_shape=(
            jax.ShapeDtypeStruct((ROWS, IDXH // NC, DIM), F32),
            jax.ShapeDtypeStruct((KEYS // NH, DIM), F32),
        ),
        in_specs=[hbm, hbm, hbm, smem, hbm, hbm, hbm],
        out_specs=(vmem, vmem),
        scratch_shapes=[
            pltpu.VMEM((ROWS, HL, LAT), BF16),
            pltpu.VMEM((NH, HL, LAT), BF16),
            pltpu.VMEM((16, 9, ROWS, WIDE), BF16),
            pltpu.VMEM((16, 8, ROWS, DIM), BF16),
            pltpu.VMEM((NH, HL, NC * ROWS), F32),
            pltpu.VMEM((16, HEADS, DIM), F32),
            pltpu.VMEM((WIDE + DIM, KEYS), BF16),
            pltpu.VMEM((NH, IDXH, DIM), BF16),
            pltpu.VMEM((NH, IDXH, DIM), F32),
            pltpu.VMEM((IDXH * ROWS, DIM), BF16),
            pltpu.VMEM((DIM, IDXH * ROWS), BF16),
            pltpu.VMEM((ROWS, IDXH), F32),
            pltpu.VMEM((IDXH * ROWS, DIM), F32),
            pltpu.VMEM((KEYS, DIM), BF16),
            pltpu.VMEM((DIM, KEYS), BF16),
            pltpu.VMEM((IDXH * ROWS, KEYS), F32),
            pltpu.VMEM((ROWS, KEYS), F32),
            pltpu.VMEM((ROWS, KEYS), F32),
            pltpu.VMEM((16, 1, KEYS), F32),
            pltpu.VMEM((NH, 1, KEYS), F32),
            pltpu.VMEM((1, DIM), F32),
            pltpu.VMEM((NC, 1, DIM), F32),
            pltpu.VMEM((IDXH * ROWS, KEYS), BF16),
            pltpu.VMEM((NH, DIM, DIM), BF16),
            pltpu.VMEM((NH, DIM, DIM), BF16),
            pltpu.VMEM((DIM, DIM), F32),
            pltpu.VMEM((NC, 64, DIM), BF16),
            pltpu.VMEM((NC, 64, DIM), BF16),
            pltpu.VMEM((64, DIM), F32),
            dma((6,)),
            *[dma((16,))] * 6,
            dma((4, 3)),
            dma((4, 3)),
            dma((3, 3)),
            dma((3, 3)),
            dma((3,)),
            dma((3,)),
            dma((8,)),
            dma((8,)),
            *[dma((16,))] * 6,
        ],
        compiler_params=pltpu.CompilerParams(
            collective_id=0, has_side_effects=True, vmem_limit_bytes=56 * 1024 * 1024
        ),
        name="index_grads",
    )(main_query, latent_keys.T, head_lse.T, lengths, index_query, index_key, index_weight)
    return pl.pallas_call(
        finish,
        out_shape=(
            jax.ShapeDtypeStruct((ROWS, IDXH // NC, DIM), F32),
            jax.ShapeDtypeStruct((KEYS // NH, DIM), F32),
        ),
        in_specs=[vmem, vmem],
        out_specs=(vmem, vmem),
        name="finish",
    )(out_query, out_key)


def solution(mesh):
    placed = (
        P("context", "heads", None),
        P("context", None),
        P(None, "heads"),
        P(),
        P("heads", None, None),
        P("context", None),
        P("heads", None),
    )
    return jax.shard_map(
        on_device,
        mesh=mesh,
        in_specs=placed,
        out_specs=(P("heads", "context", None), P(("context", "heads"), None)),
        check_vma=False,
    )
```
